32 devices in a mesh: clu: 8 (over z, y), grp: 4 (over x, core).
Axes of the slice: x: 2, y: 2, z: 4, core: 2. Of those that a mesh axis runs over, the one named last changes fastest.
Arguments:
- embeddings: bfloat16 [16384, 768], P(('clu', 'grp')), may hold values from -6 to 6
- cluster_of: int32 [16384], P(('clu', 'grp')), may hold values from 0 to 15, as said below
- new_rows: bfloat16 [512, 768], P(('clu', 'grp')), may hold values from -6 to 6
- centroids: bfloat16 [8192, 768], P(('clu', 'grp')), may hold values from -6 to 6
Outputs:
- dup_score: float32 [16384], P(('clu', 'grp'))
- centroid_score: float32 [512], P(('clu', 'grp'))
The draws below stay inside these ranges and needn't reach their ends.
Inputs may be any that keep to these rules, and one draw needn't show every extreme that they name: `cluster_of`: cluster k is owned by owner k mod 8; among the 512 rows of one device, at most 128 rows belong to the clusters of one owner, and in every such block some owner has exactly 128.
All inputs are finite; a program needn't handle non-finite values.
Results may differ from the reference program's by a relative error of at most 0.0015.
Values may be sent and summed in bfloat16 or wider, within the bound.
A program may use at most 64 MiB of HBM per device.

```python
import jax
import jax.numpy as jnp
from jax import lax

D = 768
TOK_DEV = 512
CPO = 2
CAP = 128
ROWS = 16384
NEW = 512
CENT_DEV = 256
CENTROIDS = 8192
N_CLU = 8
N_GRP = 4


def draw_cluster_of(key, part):
    slot_cap = 2 * TOK_DEV // N_CLU
    slot_total = N_CLU * slot_cap

    def one_block(block_key):
        subkeys = jax.random.split(block_key, 4)
        forced = jax.random.randint(subkeys[0], (), 0, N_CLU)
        shuffled = jax.random.permutation(subkeys[1], slot_total)
        position = jnp.argsort(shuffled).astype(jnp.int32)
        slot_ids = jnp.arange(slot_total, dtype=jnp.int32)
        priority = jnp.where(slot_ids // slot_cap == forced, slot_ids - slot_total, position)
        chosen = jnp.argsort(priority)[:TOK_DEV].astype(jnp.int32)
        owner_ids = chosen // slot_cap
        within = jax.random.randint(subkeys[2], (TOK_DEV,), 0, CPO)
        clusters = owner_ids + N_CLU * within
        return jax.random.permutation(subkeys[3], clusters)
    block_keys = jax.vmap(lambda index_value: jax.random.fold_in(key, index_value))(jnp.arange(N_CLU * N_GRP))
    return jax.vmap(one_block)(block_keys).reshape(-1).astype(jnp.int32)


def shard_levels(own_key, shape, pieces, low, largest):
    def one(dim, shards_of):
        draws = jax.random.uniform(jax.random.fold_in(jax.random.fold_in(own_key, 6), dim), (shards_of,), jnp.float32, low / len(pieces), largest / len(pieces))
        return jnp.repeat(jnp.exp(draws), shape[dim] // shards_of).reshape((-1,) + (1,) * (len(shape) - dim - 1))

    gain = one(*pieces[0])
    for cut in pieces[1:]:
        gain = gain * one(*cut)
    return gain


def gaussian(stream_key, dims, width, most, pieces=(), kind=jnp.bfloat16):
    array = width * jax.random.normal(stream_key, dims, jnp.float32)
    if pieces:
        array = array * shard_levels(stream_key, dims, pieces, -0.22, 0.18)
    return jnp.clip(array, -most, most).astype(kind)


def setup_inputs(seed: int = 0) -> dict:
    key_list = jax.random.split(jax.random.key(seed), 5)
    return {
        "embeddings": gaussian(key_list[0], (ROWS, D), 1.0, 6.0, ((0, 32),)),
        "cluster_of": draw_cluster_of(jax.random.fold_in(key_list[4], 71), 0),
        "new_rows": gaussian(key_list[2], (NEW, D), 1.0, 6.0, ((0, 32),)),
        "centroids": gaussian(key_list[3], (CENTROIDS, D), 1.0, 6.0, ((0, 32),)),
    }


epsilon = 1e-06

def normalize(values):
    wide = values.astype(jnp.float32)
    total = lax.optimization_barrier(jnp.sum(wide * wide, axis=-1, keepdims=True))
    return (wide * lax.rsqrt(total + epsilon)).astype(jnp.bfloat16)

def reference(embeddings, cluster_of, new_rows, centroids):
    normed = normalize(embeddings)
    row_total = normed.shape[0]
    capacity = CAP * N_CLU * N_GRP
    owners = cluster_of % N_CLU
    ordering = jnp.argsort(owners, stable=True).astype(jnp.int32)
    per_owner = lax.optimization_barrier(jnp.sum((owners[None, :] == jnp.arange(N_CLU, dtype=jnp.int32)[:, None]).astype(jnp.int32), axis=1))
    offsets = (jnp.cumsum(per_owner) - per_owner).astype(jnp.int32)
    padded = jnp.concatenate([ordering, jnp.full((capacity,), row_total, jnp.int32)])
    diagonal = jnp.eye(capacity, dtype=bool)

    def one_owner(owner_idx):
        indices = lax.dynamic_slice(padded, (offsets[owner_idx],), (capacity,))
        is_valid = jnp.arange(capacity, dtype=jnp.int32) < per_owner[owner_idx]
        clamped = jnp.minimum(indices, row_total - 1)
        member_units = normed[clamped]
        member_cluster = jnp.where(is_valid, cluster_of[clamped], -1)
        scores = jnp.dot(member_units, member_units.T, preferred_element_type=jnp.float32)
        matched = (member_cluster[:, None] == member_cluster[None, :]) & is_valid[:, None] & jnp.logical_not(diagonal)
        best_match = lax.optimization_barrier(jnp.max(jnp.where(matched, scores, -1.0), axis=1))
        return (jnp.where(is_valid, indices, row_total), best_match)
    target_rows, maxima = lax.map(one_owner, jnp.arange(N_CLU, dtype=jnp.int32))
    dup_score = jnp.zeros((row_total + 1,), jnp.float32).at[target_rows.reshape(-1)].set(maxima.reshape(-1))[:row_total]
    new_unit = normalize(new_rows)
    cent_unit = normalize(centroids).reshape(-1, CENT_DEV, new_rows.shape[1])

    def absorb(running, block_units):
        scores = jnp.dot(new_unit, block_units.T, preferred_element_type=jnp.float32)
        return (jnp.maximum(running, lax.optimization_barrier(jnp.max(scores, axis=1))), None)
    start_value = jnp.full((new_unit.shape[0],), -jnp.inf, jnp.float32)
    centroid_score, unused = lax.scan(absorb, start_value, cent_unit)
    return (dup_score, centroid_score)
```

```python
import functools

import jax
import jax.numpy as jnp
from jax import lax
from jax.experimental import pallas as pl
from jax.experimental.pallas import tpu as pltpu
from jax.sharding import PartitionSpec as P

epsilon = 1e-06
lanes = 128
send_chunks = 8
held_chunks = 2 * send_chunks
stage_count = held_chunks // 2
stage_rows = 2 * lanes
held_rows = held_chunks * lanes
spots_own = (0, 1, 2, 12)
spots_near = (3, 5, 7, 9)
spots_middle = (4, 6, 8, 10)
spots_outer = (11, 13, 14, 15)
MESH = pl.DeviceIdType.MESH


def normalize(values):
    wide = values.astype(jnp.float32)
    total = jnp.sum(wide * wide, axis=-1, keepdims=True)
    return (wide * lax.rsqrt(total + epsilon)).astype(jnp.bfloat16)


def pair_scores(left_units, right_units):
    return lax.dot_general(
        left_units, right_units, (((1,), (1,)), ((), ())), preferred_element_type=jnp.float32
    )


def exchange_kernel(
    clu_count,
    cap,
    new_count,
    emb_hbm,
    cluster_hbm,
    new_hbm,
    cent_hbm,
    dup_ref,
    best_ref,
    emb_ref,
    cluster_ref,
    new_ref,
    cent_ref,
    units,
    send_ref,
    relay_ref,
    ids_ref,
    held,
    held_ids,
    marks,
    id_rows,
    acc,
    new_all,
    cent_unit,
    part,
    part_in,
    best_out,
    best_in,
    message,
    message_in,
    local_sem,
    data_send,
    data_recv,
    hop_send,
    hop_recv,
    id_send,
    id_recv,
    fwd_send,
    fwd_recv,
    fwd_id_send,
    fwd_id_recv,
    new_send,
    new_recv,
    part_send,
    part_recv,
    best_send,
    best_recv,
    msg_send,
    msg_recv,
    cent_send,
    cent_recv,
):
    per_chunk = lanes // cap
    pieces = 2 if cap >= 32 else 1
    piece = cap // pieces
    cent_count = cent_hbm.shape[0]
    quarter = clu_count // 4
    codes = 2 * quarter
    group_chunks = send_chunks // 2
    group_rows = clu_count * new_count
    best_rows = group_rows // lanes
    me = lax.axis_index("clu")
    grp = lax.axis_index("grp")
    layer = me // quarter
    rest = me % quarter
    half = grp // 2
    inner = (layer == 1) | (layer == 2)
    outer = jnp.logical_not(inner)
    inner_bit = inner.astype(jnp.int32)
    self_place = codes

    def remote(src, dst, send_sem, recv_sem, device):
        return pltpu.make_async_remote_copy(
            src_ref=src,
            dst_ref=dst,
            send_sem=send_sem,
            recv_sem=recv_sem,
            device_id=device,
            device_id_type=MESH,
        )

    def far(step):
        return {"clu": me ^ step, "grp": grp}

    def near(step):
        return {"clu": me, "grp": grp ^ step}

    def related(to_layer, code):
        return {
            "clu": to_layer * quarter + (rest ^ (code // 2)),
            "grp": grp ^ (2 * (code % 2)),
        }

    first_layer = jnp.where(inner, layer ^ 3, layer ^ 1)
    second_layer = jnp.where(inner, layer, layer ^ 2)

    def owner_device(place):
        part_of, code = divmod(place, codes)
        return related(second_layer if part_of else first_layer, code)

    def owner_block(place):
        chunk, within = divmod(place, per_chunk)
        part_of, step = divmod(chunk, group_chunks)
        if part_of:
            spot = jnp.where(inner, spots_own[step], spots_outer[step])
        else:
            spot = jnp.where(inner, spots_middle[step], spots_near[step])
        return spot * per_chunk + within

    def held_source(spot):
        for to_layer, spots, part_of in (
            (layer, spots_own, 1),
            (layer ^ 1, spots_near, 0),
            (layer ^ 3, spots_middle, 0),
            (layer ^ 2, spots_outer, 1),
        ):
            if spot in spots:
                return to_layer, part_of * group_chunks + spots.index(spot)

    barrier = pltpu.get_barrier_semaphore()

    def greet(device):
        pl.semaphore_signal(barrier, inc=1, device_id=device, device_id_type=MESH)

    for step in range(1, clu_count):
        greet(far(step))
    for step in (1, 2, 3):
        greet(near(step))
    greeted = clu_count - 1 + 3
    for quarter_step in (0, 1, 2):
        for step in range(quarter):
            if quarter_step or step:
                greet({"clu": me ^ (quarter_step * quarter + step), "grp": grp ^ 2})
                greeted += 1

    @pl.when(inner)
    def _():
        for step in range(quarter):
            greet({"clu": me ^ (3 * quarter + step), "grp": grp ^ 2})

    local = [
        pltpu.make_async_copy(cluster_hbm, cluster_ref, local_sem.at[0]),
        pltpu.make_async_copy(emb_hbm, emb_ref, local_sem.at[1]),
        pltpu.make_async_copy(new_hbm, new_ref, local_sem.at[2]),
    ]
    for copy in local:
        copy.start()
    local_cent = pltpu.make_async_copy(
        cent_hbm, cent_ref.at[pl.ds(0, cent_count)], local_sem.at[3]
    )
    pl.when(outer)(local_cent.start)

    local[0].wait()
    cluster = cluster_ref[...]
    rows = cluster.shape[1]
    owner = cluster & (clu_count - 1)
    owner_layer = 1 + owner // codes
    second = (owner_layer == second_layer).astype(jnp.int32)
    place = second * codes + ((owner % codes) ^ (2 * rest + half))
    owner_hot = lax.broadcasted_iota(jnp.int32, (clu_count, rows), 0) == place
    before = lax.broadcasted_iota(jnp.int32, (rows, rows), 0) < lax.broadcasted_iota(
        jnp.int32, (rows, rows), 1
    )
    preceding = jnp.dot(
        owner_hot.astype(jnp.bfloat16),
        before.astype(jnp.bfloat16),
        preferred_element_type=jnp.float32,
    )
    rank = jnp.sum(jnp.where(owner_hot, preceding, 0.0), axis=0, keepdims=True).astype(jnp.int32)
    slot = place * cap + rank
    id_values = jnp.broadcast_to((cluster + 1).astype(jnp.float32), (8, rows)).astype(jnp.bfloat16)
    chunk_slot = lax.broadcasted_iota(jnp.int32, (lanes, rows), 0)
    inner_block = lax.broadcasted_iota(jnp.int32, (1, lanes), 1) // cap
    local[1].wait()
    units[...] = normalize(emb_ref[...])
    for chunk in range(send_chunks):
        chosen = (chunk_slot + chunk * lanes == slot).astype(jnp.bfloat16)
        packed = jnp.dot(chosen, units[...], preferred_element_type=jnp.float32)
        send_ref[chunk * lanes : (chunk + 1) * lanes, :] = packed.astype(jnp.bfloat16)
        tile = pair_scores(id_values, chosen)[0:1]
        for within in range(per_chunk):
            own = tile if per_chunk == 1 else jnp.where(inner_block == within, tile, 0.0)
            ids_ref[chunk * per_chunk + within] = own
    local[2].wait()
    new_all[0, 0:new_count, :] = normalize(new_ref[...])

    @pl.when(inner)
    def _():
        pl.semaphore_wait(barrier, greeted + quarter)

    @pl.when(outer)
    def _():
        pl.semaphore_wait(barrier, greeted)

    def new_slots(start, count):
        return new_all.at[0, pl.ds(start * new_count, count * new_count)]

    def layer_new(step):
        return remote(
            new_slots(0, 1),
            new_slots(step, 1),
            new_send.at[step - 1],
            new_recv.at[step - 1],
            far(step * quarter),
        )

    rest_steps = quarter.bit_length() - 1

    def rest_new(index):
        count = 4 << index
        return remote(
            new_slots(0, count),
            new_slots(count, count),
            new_send.at[3 + index],
            new_recv.at[3 + index],
            far(1 << index),
        )

    wide_base = 3 + rest_steps

    def wide_new(index):
        src, dst, step = ((0, 2, 2), (0, 1, 1), (2, 3, 1))[index]
        return remote(
            new_all.at[src],
            new_all.at[dst],
            new_send.at[wide_base + index],
            new_recv.at[wide_base + index],
            near(step),
        )

    cent_copy = remote(
        cent_hbm,
        cent_ref.at[pl.ds(cent_count, cent_count)],
        cent_send.at[0],
        cent_recv.at[0],
        far(quarter),
    )

    def piece_rows(place, index):
        return pl.ds(place * cap + index * piece, piece)

    def landing(place, index):
        block = owner_block(place)
        row = pl.multiple_of(block * cap + index * piece, piece)
        return held.at[pl.ds(row, piece)], data_recv.at[block * pieces + index]

    def direct_copy(place, index):
        target, arrived = landing(place, index)
        return remote(
            send_ref.at[piece_rows(place, index)],
            target,
            data_send.at[place * pieces + index],
            arrived,
            owner_device(place),
        )

    def hop_copy(place, index):
        return remote(
            send_ref.at[piece_rows(place, index)],
            relay_ref.at[piece_rows(place, index)],
            hop_send.at[place * pieces + index],
            hop_recv.at[place * pieces + index],
            related(layer, place % codes),
        )

    def relay_copy(place, index):
        target, arrived = landing(place, index)
        return remote(
            relay_ref.at[piece_rows(place, index)],
            target,
            data_send.at[place * pieces + index],
            arrived,
            related(second_layer if place >= codes else first_layer, 0),
        )

    def id_copy(place):
        block = owner_block(place)
        return remote(
            ids_ref.at[place],
            held_ids.at[block],
            id_send.at[place],
            id_recv.at[block],
            owner_device(place),
        )

    def send_direct(place):
        for index in range(pieces):
            direct_copy(place, index).start()

    def send_hop(place):
        for index in range(pieces):
            hop_copy(place, index).start()

    def relay(place):
        for index in range(pieces):
            hop_copy(place, index).wait_recv()
            relay_copy(place, index).start()

    late_place = self_place + (group_chunks - 1) * per_chunk

    def part_copy(step):
        return remote(
            part.at[step],
            part_in.at[step - 1],
            part_send.at[step - 1],
            part_recv.at[step - 1],
            near(step),
        )

    def best_copy(step):
        return remote(
            best_out,
            best_in.at[step],
            best_send.at[step],
            best_recv.at[step],
            far(step),
        )

    def score_new():
        for step in range(4):
            scores = pair_scores(cent_unit[...], new_all[step])
            top = jnp.max(scores.reshape(scores.shape[0] // 8, 8, group_rows), axis=0)
            top = jnp.max(top, axis=0, keepdims=True)
            for row in range(best_rows):
                part[step, row : row + 1, :] = top[:, row * lanes : (row + 1) * lanes]
        for step in (1, 2, 3):
            part_copy(step).start()

    def spread_best():
        best = part[0]
        for step in (1, 2, 3):
            part_copy(step).wait_recv()
            best = jnp.maximum(best, part_in[step - 1])
        best_out[...] = best
        for step in range(1, clu_count):
            best_copy(step).start()

    def held_copy(block, index):
        return remote(
            send_ref.at[pl.ds(0, piece)],
            held.at[pl.ds(block * cap + index * piece, piece)],
            data_send.at[0],
            data_recv.at[block * pieces + index],
            near(1),
        )

    def held_id_copy(block):
        return remote(
            ids_ref.at[0], held_ids.at[block], id_send.at[0], id_recv.at[block], near(1)
        )

    def forward(spot):
        return (
            remote(
                held_ids.at[pl.ds(spot * per_chunk, per_chunk)],
                held_ids.at[pl.ds((held_chunks + spot) * per_chunk, per_chunk)],
                fwd_id_send.at[spot],
                fwd_id_recv.at[spot],
                near(1),
            ),
            remote(
                held.at[pl.ds(spot * lanes, lanes)],
                held.at[pl.ds(held_rows + spot * lanes, lanes)],
                fwd_send.at[spot],
                fwd_recv.at[spot],
                near(1),
            ),
        )

    def spread_marks(spot):
        row = held_ids[spot * per_chunk]
        for within in range(1, per_chunk):
            row = row + held_ids[spot * per_chunk + within]
        marks[pl.ds(spot * lanes, lanes), :] = jnp.transpose(
            jnp.broadcast_to(row, (lanes, lanes))
        )
        if spot < held_chunks:
            stage, part_of = divmod(spot, 2)
            id_rows[stage, :, pl.ds(part_of * lanes, lanes)] = jnp.broadcast_to(row, (8, lanes))

    def pass_on(spot):
        for within in range(per_chunk):
            block = spot * per_chunk + within
            if block > 0:
                held_id_copy(block).wait_recv()
                for index in range(pieces):
                    held_copy(block, index).wait_recv()
        for copy in forward(spot):
            copy.start()
        spread_marks(spot)

    def receive(spot):
        for copy in forward(spot):
            copy.wait_recv()
        spread_marks(held_chunks + spot)

    def tile_pair(start, count, right, diagonal=False):
        if not isinstance(start, int):
            start = pl.multiple_of(start, count)
        left_rows = pl.ds(start, count)
        right_start = right * stage_rows
        if not isinstance(right_start, int):
            right_start = pl.multiple_of(right_start, stage_rows)
        mark = marks[left_rows, :]
        matched = jnp.concatenate([mark, mark], axis=1) == id_rows[right][0:1]
        if diagonal:
            row_id = lax.broadcasted_iota(jnp.int32, (stage_rows, stage_rows), 0)
            col_id = lax.broadcasted_iota(jnp.int32, (stage_rows, stage_rows), 1)
            matched = matched & (row_id != col_id)
        scores = pair_scores(held[left_rows, :], held[pl.ds(right_start, stage_rows), :])
        kept = jnp.where(matched, scores, -1.0)
        top = jnp.max(kept.reshape(count // 8, 8, stage_rows), axis=0)
        acc[right] = jnp.maximum(acc[right], top)

    def stage_diagonal(stage):
        tile_pair(stage * stage_rows, stage_rows, stage, diagonal=True)
        tile_pair(held_rows + stage * stage_rows, stage_rows, stage)

    def compute(stage):
        stage_diagonal(stage)

        def body(other, carry):
            tile_pair(stage * stage_rows, stage_rows, other)
            tile_pair(held_rows + stage * stage_rows, stage_rows, other)
            tile_pair(other * stage_rows, stage_rows, stage)
            tile_pair(held_rows + other * stage_rows, stage_rows, stage)
            return carry

        if stage:
            lax.fori_loop(0, stage, body, 0)

    def take(stage):
        pass_on(2 * stage)
        pass_on(2 * stage + 1)
        receive(2 * stage)
        receive(2 * stage + 1)

    last = stage_count - 1

    def chunk_rows(spot):
        def body(other, carry):
            tile_pair(spot * lanes, lanes, other)
            tile_pair(held_rows + spot * lanes, lanes, other)
            return carry

        lax.fori_loop(0, last, body, 0)

    def last_columns():
        def body(other, carry):
            tile_pair(other * stage_rows, stage_rows, last)
            tile_pair(held_rows + other * stage_rows, stage_rows, last)
            return carry

        lax.fori_loop(0, last, body, 0)

    def message_copy(block):
        spot, within = divmod(block, per_chunk)
        to_layer, chunk = held_source(spot)
        place = chunk * per_chunk + within
        return remote(
            message.at[spot],
            message_in.at[place],
            msg_send.at[block],
            msg_recv.at[place],
            related(to_layer, place % codes),
        )

    def message_copy_in(place):
        return remote(
            message.at[0], message_in.at[place], msg_send.at[0], msg_recv.at[place], near(1)
        )

    @pl.when(inner)
    def _():
        for step in (1, 2):
            layer_new(step).start()
        for place in range(clu_count):
            if place != self_place:
                id_copy(place).start()
        for code in range(codes):
            send_direct(code)
            if code and self_place + code < late_place:
                send_direct(self_place + code)
        cent_copy.start()
        held[0:cap, :] = send_ref[self_place * cap : (self_place + 1) * cap, :]
        held_ids[0] = ids_ref[self_place]
        acc[...] = jnp.full(acc.shape, -1.0, jnp.float32)
        for stage in range(last):
            pass_on(2 * stage)
            if 2 * stage == spots_middle[-1]:
                for place in range(late_place, clu_count):
                    send_direct(place)
            pass_on(2 * stage + 1)
            receive(2 * stage)
            receive(2 * stage + 1)
            compute(stage)
        pass_on(2 * last)
        receive(2 * last)
        chunk_rows(2 * last)
        pass_on(2 * last + 1)
        receive(2 * last + 1)
        chunk_rows(2 * last + 1)
        stage_diagonal(last)
        last_columns()
        for stage in range(stage_count):
            final = jnp.max(acc[stage], axis=0, keepdims=True)
            for part_of in range(2):
                message[2 * stage + part_of] = final[:, part_of * lanes : (part_of + 1) * lanes]
        for block in range(1, 2 * clu_count):
            message_copy(block).start()
        message_in[self_place] = message[0]
        for spot in range(held_chunks):
            for copy in forward(spot):
                copy.wait_send()
        cent_copy.wait_send()
        for step in (1, 2):
            layer_new(step).wait_send()
        for place in range(clu_count):
            if place != self_place:
                id_copy(place).wait_send()
                for index in range(pieces):
                    direct_copy(place, index).wait_send()
        for step in range(1, clu_count):
            if step // quarter in (1, 2):
                best_copy(step).wait_recv()
        for block in range(1, 2 * clu_count):
            message_copy(block).wait_send()

    @pl.when(outer)
    def _():
        layer_new(3).start()
        for place in range(clu_count):
            id_copy(place).start()
        send_direct(0)
        for code in range(1, codes):
            send_hop(code)
        local_cent.wait()
        cent_unit[0:cent_count, :] = normalize(cent_ref[0:cent_count, :])
        for code in range(1, codes // 2 + 1):
            relay(code)
        for step in (1, 2, 3):
            layer_new(step).wait_recv()
        if rest_steps:
            rest_new(0).start()
        for code in range(codes // 2 + 1, codes):
            relay(code)
        send_direct(codes)
        for code in range(1, codes):
            send_hop(codes + code)
        for index in range(rest_steps):
            rest_new(index).wait_recv()
            if index + 1 < rest_steps:
                rest_new(index + 1).start()
        wide_new(0).start()
        for code in range(1, codes):
            relay(codes + code)
        cent_copy.wait_recv()
        cent_unit[cent_count:, :] = normalize(cent_ref[cent_count:, :])
        wide_new(0).wait_recv()
        wide_new(1).start()
        wide_new(2).start()
        wide_new(1).wait_recv()
        wide_new(2).wait_recv()
        score_new()
        spread_best()
        layer_new(3).wait_send()
        for index in range(rest_steps):
            rest_new(index).wait_send()
        for index in range(3):
            wide_new(index).wait_send()
        for step in (1, 2, 3):
            part_copy(step).wait_send()
        for step in range(1, clu_count):
            best_copy(step).wait_send()
            if step // quarter == 3 or step // quarter == 0:
                best_copy(step).wait_recv()
        for place in range(clu_count):
            id_copy(place).wait_send()
            for index in range(pieces):
                if place % codes:
                    hop_copy(place, index).wait_send()
                    relay_copy(place, index).wait_send()
                else:
                    direct_copy(place, index).wait_send()
        message_copy_in(self_place).wait_recv()

    def best_piece(source, step):
        layer_step, rest_step = divmod(step, quarter)
        start = (rest_step * 4 + layer_step) * new_count
        row = start // lanes
        return source[row : row + 1, start % lanes : start % lanes + new_count]

    @pl.when(inner)
    def _():
        best = None
        for step in range(quarter, 3 * quarter):
            found = best_piece(best_in[step], step)
            best = found if best is None else jnp.maximum(best, found)
        best_ref[...] = best

    @pl.when(outer)
    def _():
        best = best_piece(best_out[...], 0)
        for step in (*range(1, quarter), *range(3 * quarter, clu_count)):
            best = jnp.maximum(best, best_piece(best_in[step], step))
        best_ref[...] = best

    for place in range(clu_count):
        if place != self_place:
            message_copy_in(place).wait_recv()

    row_list = []
    for chunk in range(send_chunks):
        row = message_in[chunk * per_chunk]
        for within in range(1, per_chunk):
            row = jnp.where(inner_block == within, message_in[chunk * per_chunk + within], row)
        row_list.append(row)
    columns = jnp.transpose(
        jnp.concatenate([jnp.broadcast_to(row, (16, lanes)) for row in row_list], axis=0)
    )
    total = jnp.zeros(slot.shape, jnp.float32)
    for chunk in range(send_chunks):
        column = columns[:, chunk * 16 : chunk * 16 + 1]
        total = total + jnp.sum(
            jnp.where(chunk_slot + chunk * lanes == slot, column, 0.0), axis=0, keepdims=True
        )
    dup_ref[...] = total


def shards(embeddings, cluster_of, new_rows, centroids):
    clu_count = lax.axis_size("clu")
    rows, width = embeddings.shape
    new_count = new_rows.shape[0]
    cap = 2 * rows // clu_count
    slots = clu_count * cap
    assert slots == send_chunks * lanes
    assert lax.axis_size("grp") == 4
    vmem = pl.BlockSpec(memory_space=pltpu.VMEM)
    anywhere = pl.BlockSpec(memory_space=pl.ANY)
    dma = pltpu.SemaphoreType.DMA
    group_rows = clu_count * new_count
    best_rows = group_rows // lanes
    cent_count = centroids.shape[0]
    new_steps = 3 + (clu_count // 4).bit_length() - 1 + 3
    dup, best = pl.pallas_call(
        functools.partial(exchange_kernel, clu_count, cap, new_count),
        out_shape=(
            jax.ShapeDtypeStruct((1, rows), jnp.float32),
            jax.ShapeDtypeStruct((1, new_count), jnp.float32),
        ),
        in_specs=[anywhere] * 4,
        out_specs=(vmem, vmem),
        scratch_shapes=[
            pltpu.VMEM((rows, width), jnp.bfloat16),
            pltpu.VMEM((1, rows), jnp.int32),
            pltpu.VMEM((new_count, width), jnp.bfloat16),
            pltpu.VMEM((2 * cent_count, width), jnp.bfloat16),
            pltpu.VMEM((rows, width), jnp.bfloat16),
            pltpu.VMEM((slots, width), jnp.bfloat16),
            pltpu.VMEM((slots, width), jnp.bfloat16),
            pltpu.VMEM((clu_count, 1, lanes), jnp.float32),
            pltpu.VMEM((2 * held_rows, width), jnp.bfloat16),
            pltpu.VMEM((4 * clu_count, 1, lanes), jnp.float32),
            pltpu.VMEM((2 * held_rows, lanes), jnp.float32),
            pltpu.VMEM((stage_count, 8, stage_rows), jnp.float32),
            pltpu.VMEM((stage_count, 8, stage_rows), jnp.float32),
            pltpu.VMEM((4, group_rows, width), jnp.bfloat16),
            pltpu.VMEM((2 * cent_count, width), jnp.bfloat16),
            pltpu.VMEM((4, best_rows, lanes), jnp.float32),
            pltpu.VMEM((3, best_rows, lanes), jnp.float32),
            pltpu.VMEM((best_rows, lanes), jnp.float32),
            pltpu.VMEM((clu_count, best_rows, lanes), jnp.float32),
            pltpu.VMEM((held_chunks, 1, lanes), jnp.float32),
            pltpu.VMEM((clu_count, 1, lanes), jnp.float32),
            dma((4,)),
            dma((2 * clu_count,)),
            dma((4 * clu_count,)),
            dma((2 * clu_count,)),
            dma((2 * clu_count,)),
            dma((clu_count,)),
            dma((2 * clu_count,)),
            dma((held_chunks,)),
            dma((held_chunks,)),
            dma((held_chunks,)),
            dma((held_chunks,)),
            dma((new_steps,)),
            dma((new_steps,)),
            dma((3,)),
            dma((3,)),
            dma((clu_count,)),
            dma((clu_count,)),
            dma((2 * clu_count,)),
            dma((clu_count,)),
            dma((1,)),
            dma((1,)),
        ],
        compiler_params=pltpu.CompilerParams(
            collective_id=0, has_side_effects=True, vmem_limit_bytes=67043328
        ),
        name="exchange",
    )(embeddings, cluster_of.reshape(1, rows), new_rows, centroids)
    return (dup.reshape(rows), best.reshape(new_count))


def solution(mesh):
    return jax.shard_map(
        shards,
        mesh=mesh,
        in_specs=(
            P(("clu", "grp"), None),
            P(("clu", "grp")),
            P(("clu", "grp"), None),
            P(("clu", "grp"), None),
        ),
        out_specs=(P(("clu", "grp")), P(("clu", "grp"))),
        check_vma=False,
    )
```

```python
import functools

import jax
import jax.numpy as jnp
from jax import lax
from jax.experimental import pallas as pl
from jax.experimental.pallas import tpu as pltpu
from jax.sharding import PartitionSpec as P

epsilon = 1e-06
lanes = 128
chunk_order = (0, 1, 2, 3, 4, 5, 6, 7)
chunk_count = len(chunk_order)
stage_count = chunk_count // 2
MESH = pl.DeviceIdType.MESH


def normalize(values):
    wide = values.astype(jnp.float32)
    total = jnp.sum(wide * wide, axis=-1, keepdims=True)
    return (wide * lax.rsqrt(total + epsilon)).astype(jnp.bfloat16)


def pair_scores(left_units, right_units):
    return lax.dot_general(
        left_units, right_units, (((1,), (1,)), ((), ())), preferred_element_type=jnp.float32
    )


def exchange_kernel(
    clu_count,
    cap,
    new_count,
    emb_hbm,
    cluster_hbm,
    new_hbm,
    cent_hbm,
    dup_ref,
    best_ref,
    emb_ref,
    cluster_ref,
    new_ref,
    cent_ref,
    units,
    send_ref,
    ids_ref,
    held,
    held_ids,
    marks,
    id_rows,
    own_acc,
    mate_acc,
    mate_in,
    new_held,
    cent_unit,
    part,
    part_in,
    message,
    message_in,
    local_sem,
    data_send,
    data_recv,
    id_send,
    id_recv,
    new_send,
    new_recv,
    fwd_send,
    fwd_recv,
    fwd_id_send,
    fwd_id_recv,
    wide_send,
    wide_recv,
    part_send,
    part_recv,
    mate_send,
    mate_recv,
    msg_send,
    msg_recv,
):
    per_chunk = clu_count // chunk_count
    half = lanes
    stage_rows = 2 * half
    me = lax.axis_index("clu")
    grp = lax.axis_index("grp")

    def far(block):
        chunk, inner = divmod(block, per_chunk)
        return {"clu": me ^ (chunk_order[chunk] * per_chunk + inner), "grp": grp}

    def near(step):
        return {"clu": me, "grp": grp ^ step}

    def chunk_row(chunk, kind):
        stage, part_of = divmod(chunk, 2)
        return stage * 3 * stage_rows + kind * stage_rows + part_of * half

    def block_rows(block):
        chunk, inner = divmod(block, per_chunk)
        return pl.ds(chunk_row(chunk, 0) + inner * cap, cap)

    def remote(src, dst, send_sem, recv_sem, device):
        return pltpu.make_async_remote_copy(
            src_ref=src,
            dst_ref=dst,
            send_sem=send_sem,
            recv_sem=recv_sem,
            device_id=device,
            device_id_type=MESH,
        )

    barrier = pltpu.get_barrier_semaphore()
    for block in range(1, clu_count):
        pl.semaphore_signal(barrier, inc=1, device_id=far(block), device_id_type=MESH)
    for step in (1, 2, 3):
        pl.semaphore_signal(barrier, inc=1, device_id=near(step), device_id_type=MESH)

    local = [
        pltpu.make_async_copy(new_hbm, new_ref, local_sem.at[0]),
        pltpu.make_async_copy(cluster_hbm, cluster_ref, local_sem.at[1]),
        pltpu.make_async_copy(emb_hbm, emb_ref, local_sem.at[2]),
        pltpu.make_async_copy(cent_hbm, cent_ref, local_sem.at[3]),
    ]
    for copy in local:
        copy.start()

    new_copies = []
    data_copies = [None]
    id_copies = [None]
    for block in range(1, clu_count):
        new_copies.append(
            remote(
                new_held.at[0, pl.ds(0, new_count)],
                new_held.at[0, pl.ds(block * new_count, new_count)],
                new_send.at[block],
                new_recv.at[block],
                far(block),
            )
        )
        id_copies.append(
            remote(
                ids_ref.at[block],
                held_ids.at[0, block],
                id_send.at[block],
                id_recv.at[block],
                far(block),
            )
        )
        data_copies.append(
            remote(
                send_ref.at[pl.ds(block * cap, cap)],
                held.at[block_rows(block)],
                data_send.at[block],
                data_recv.at[block],
                far(block),
            )
        )

    local[0].wait()
    new_held[0, 0:new_count, :] = normalize(new_ref[...])
    local[1].wait()
    cluster = cluster_ref[...]
    rows = cluster.shape[1]
    distance = (cluster & (clu_count - 1)) ^ me
    far_chunk = distance // per_chunk
    place = jnp.zeros_like(distance)
    for index, chunk in enumerate(chunk_order):
        place = jnp.where(far_chunk == chunk, index, place)
    place = place * per_chunk + distance % per_chunk
    owner_hot = lax.broadcasted_iota(jnp.int32, (clu_count, rows), 0) == place
    before = lax.broadcasted_iota(jnp.int32, (rows, rows), 0) < lax.broadcasted_iota(
        jnp.int32, (rows, rows), 1
    )
    preceding = jnp.dot(
        owner_hot.astype(jnp.bfloat16),
        before.astype(jnp.bfloat16),
        preferred_element_type=jnp.float32,
    )
    rank = jnp.sum(jnp.where(owner_hot, preceding, 0.0), axis=0, keepdims=True).astype(jnp.int32)
    slot = place * cap + rank
    id_values = jnp.broadcast_to((cluster + 1).astype(jnp.float32), (8, rows)).astype(jnp.bfloat16)
    chunk_slot = lax.broadcasted_iota(jnp.int32, (lanes, rows), 0)
    inner_block = lax.broadcasted_iota(jnp.int32, (1, lanes), 1) // cap
    local[2].wait()
    units[...] = normalize(emb_ref[...])
    def pack(chunk):
        chosen = (chunk_slot + chunk * lanes == slot).astype(jnp.bfloat16)
        packed = jnp.dot(chosen, units[...], preferred_element_type=jnp.float32).astype(
            jnp.bfloat16
        )
        tile = pair_scores(id_values, chosen)[0:1]
        for inner in range(per_chunk):
            block = chunk * per_chunk + inner
            if per_chunk == 1:
                own_tile = tile
            else:
                own_tile = jnp.where(inner_block == inner, tile, 0.0)
            if block == 0:
                held_ids[0, 0] = own_tile
                held[block_rows(0), :] = packed[0:cap]
            else:
                ids_ref[block] = own_tile
        if per_chunk > 1 or chunk > 0:
            send_ref[chunk * lanes : (chunk + 1) * lanes, :] = packed

    def dispatch(chunk):
        for block in range(max(1, chunk * per_chunk), (chunk + 1) * per_chunk):
            id_copies[block].start()
            data_copies[block].start()

    forwards = {}

    def spread_marks(chunk, kind):
        tile = held_ids[kind, chunk * per_chunk]
        for inner in range(1, per_chunk):
            tile = tile + held_ids[kind, chunk * per_chunk + inner]
        square = jnp.broadcast_to(tile, (lanes, lanes))
        marks[pl.ds(chunk_row(chunk, kind), half), :] = jnp.transpose(square)
        if kind < 2:
            stage, part_of = divmod(chunk, 2)
            id_rows[stage, kind, :, pl.ds(part_of * half, half)] = jnp.broadcast_to(
                tile, (8, half)
            )

    def pass_on(chunk):
        for inner in range(per_chunk):
            block = chunk * per_chunk + inner
            if block > 0:
                id_copies[block].wait_recv()
                data_copies[block].wait_recv()
        src_rows = pl.ds(chunk_row(chunk, 0), half)
        src_ids = pl.ds(chunk * per_chunk, per_chunk)
        for kind in (2, 1):
            index = (kind - 1) * chunk_count + chunk
            ids = remote(
                held_ids.at[0, src_ids],
                held_ids.at[kind, src_ids],
                fwd_id_send.at[index],
                fwd_id_recv.at[index],
                near(kind),
            )
            data = remote(
                held.at[src_rows],
                held.at[pl.ds(chunk_row(chunk, kind), half)],
                fwd_send.at[index],
                fwd_recv.at[index],
                near(kind),
            )
            ids.start()
            data.start()
            forwards[chunk, kind] = (ids, data)
        spread_marks(chunk, 0)

    def receive(chunk, kinds=(1, 2)):
        for kind in kinds:
            ids, data = forwards[chunk, kind]
            ids.wait_recv()
            data.wait_recv()
            spread_marks(chunk, kind)

    def fold(scores, matched):
        kept = jnp.where(matched, scores, -1.0)
        return jnp.max(kept.reshape(stage_rows // 8, 8, stage_rows), axis=0)

    def tile_rows(stage, kind):
        start = stage * (3 * stage_rows) + kind * stage_rows
        if not isinstance(start, int):
            start = pl.multiple_of(start, stage_rows)
        return pl.ds(start, stage_rows)

    def own_pair(kind, left, right):
        rows = tile_rows(left, kind)
        mark = marks[rows, :]
        matched = jnp.concatenate([mark, mark], axis=1) == id_rows[right, 0][0:1]
        if kind == 0:
            row_id = lax.broadcasted_iota(jnp.int32, (stage_rows, stage_rows), 0)
            col_id = lax.broadcasted_iota(jnp.int32, (stage_rows, stage_rows), 1)
            matched = matched & (row_id - col_id != (right - left) * stage_rows)
        scores = pair_scores(held[rows, :], held[tile_rows(right, 0), :])
        own_acc[right] = jnp.maximum(own_acc[right], fold(scores, matched))

    def mate_pair(left, right):
        rows = tile_rows(left, 2)
        mark = marks[rows, :]
        matched = jnp.concatenate([mark, mark], axis=1) == id_rows[right, 1][0:1]
        scores = pair_scores(held[rows, :], held[tile_rows(right, 1), :])
        mate_acc[right] = jnp.maximum(mate_acc[right], fold(scores, matched))

    def compute(stage):
        receive(2 * stage)
        receive(2 * stage + 1)

        def body(step, carry):
            left = jnp.minimum(step, stage)
            right = jnp.where(step <= stage, stage, step - stage - 1)
            for kind in range(3):
                own_pair(kind, left, right)
            mate_pair(left, right)
            return carry

        lax.fori_loop(0, 2 * stage + 1, body, 0)

    def compute_last():
        last = stage_count - 1

        def own_rows(step, carry):
            own_pair(0, last, step)
            return carry

        def own_cols(step, carry):
            for kind in range(3):
                own_pair(kind, step, last)
            return carry

        def mate_rows(step, carry):
            own_pair(1, last, step)
            return carry

        def cross_rows(step, carry):
            own_pair(2, last, step)
            mate_pair(last, step)
            return carry

        def mate_cols(step, carry):
            mate_pair(step, last)
            return carry

        lax.fori_loop(0, stage_count, own_rows, 0)
        lax.fori_loop(0, last, own_cols, 0)
        receive(2 * last, (1,))
        receive(2 * last + 1, (1,))
        lax.fori_loop(0, last, mate_cols, 0)
        lax.fori_loop(0, stage_count, mate_rows, 0)
        receive(2 * last, (2,))
        receive(2 * last + 1, (2,))
        lax.fori_loop(0, stage_count, cross_rows, 0)

    group_rows = clu_count * new_count
    best_rows = group_rows // lanes
    cross_new = remote(
        new_held.at[0], new_held.at[2], wide_send.at[0], wide_recv.at[0], near(2)
    )
    mate_new = remote(new_held.at[0], new_held.at[1], wide_send.at[1], wide_recv.at[1], near(1))
    corner_new = remote(new_held.at[2], new_held.at[3], wide_send.at[2], wide_recv.at[2], near(1))
    part_copies = [
        remote(
            part.at[step],
            part_in.at[step - 1],
            part_send.at[step - 1],
            part_recv.at[step - 1],
            near(step),
        )
        for step in (1, 2, 3)
    ]

    def new_first():
        for copy in new_copies:
            copy.wait_recv()
        cross_new.start()
        mate_new.start()

    def new_second():
        cross_new.wait_recv()
        corner_new.start()

    def new_third():
        mate_new.wait_recv()
        corner_new.wait_recv()
        for step in range(4):
            scores = pair_scores(cent_unit[...], new_held[step])
            top = jnp.max(
                scores.reshape(scores.shape[0] // 8, 8, group_rows), axis=0
            )
            top = jnp.max(top, axis=0, keepdims=True)
            if group_rows == lanes:
                part[step] = jnp.broadcast_to(top, (8, lanes))
            else:
                for row in range(group_rows // lanes):
                    part[step, row : row + 1, :] = top[:, row * lanes : (row + 1) * lanes]
        for copy in part_copies:
            copy.start()

    for chunk in range(chunk_count):
        pack(chunk)
    pl.semaphore_wait(barrier, clu_count - 1 + 3)
    for copy in new_copies:
        copy.start()
    for chunk in range(chunk_count):
        dispatch(chunk)
    own_acc[...] = jnp.full(own_acc.shape, -1.0, jnp.float32)
    mate_acc[...] = jnp.full(mate_acc.shape, -1.0, jnp.float32)
    pass_on(0)
    local[3].wait()
    cent_unit[...] = normalize(cent_ref[...])
    pass_on(1)
    new_first()
    pass_on(2)
    pass_on(3)
    new_second()
    compute(0)
    pass_on(4)
    new_third()
    pass_on(5)
    compute(1)
    pass_on(6)
    compute(2)
    pass_on(7)
    compute_last()

    mate_copy = remote(mate_acc, mate_in, mate_send.at[0], mate_recv.at[0], near(1))
    mate_copy.start()
    cent_best = part[0]
    for step in (1, 2, 3):
        part_copies[step - 1].wait_recv()
        cent_best = jnp.maximum(cent_best, part_in[step - 1])
    mate_copy.wait_recv()
    for stage in range(stage_count):
        final = jnp.max(
            jnp.maximum(own_acc[stage], mate_in[stage]), axis=0, keepdims=True
        )
        for part_of in range(2):
            message[2 * stage + part_of, 0:1, :] = final[:, part_of * half : (part_of + 1) * half]
            message[2 * stage + part_of, 1:, :] = cent_best[0:best_rows]
    messages = []
    for block in range(1, clu_count):
        copy = remote(
            message.at[block // per_chunk],
            message_in.at[block],
            msg_send.at[block],
            msg_recv.at[block],
            far(block),
        )
        copy.start()
        messages.append(copy)
    message_in[0] = message[0]
    for block in range(1, clu_count):
        new_copies[block - 1].wait_send()
        id_copies[block].wait_send()
        data_copies[block].wait_send()
    for ids, data in forwards.values():
        ids.wait_send()
        data.wait_send()
    for copy in (cross_new, mate_new, corner_new, mate_copy, *part_copies):
        copy.wait_send()
    for copy in messages:
        copy.wait()

    lane_block = lax.broadcasted_iota(jnp.int32, (1, lanes), 1) // cap
    row_list = []
    for chunk in range(chunk_count):
        row = message_in[chunk * per_chunk, 0:1, :]
        for inner in range(1, per_chunk):
            row = jnp.where(lane_block == inner, message_in[chunk * per_chunk + inner, 0:1, :], row)
        row_list.append(row)
    columns = jnp.transpose(
        jnp.concatenate([jnp.broadcast_to(row, (16, lanes)) for row in row_list], axis=0)
    )
    total = jnp.zeros(slot.shape, jnp.float32)
    position = lax.broadcasted_iota(jnp.int32, (lanes, slot.shape[1]), 0)
    for chunk in range(chunk_count):
        column = columns[:, chunk * 16 : chunk * 16 + 1]
        total = total + jnp.sum(
            jnp.where(position + chunk * lanes == slot, column, 0.0), axis=0, keepdims=True
        )
    dup_ref[...] = total
    best = None
    for block in range(clu_count):
        start = block * new_count
        row = 1 + start // lanes
        piece = message_in[block, row : row + 1, :][:, start % lanes : start % lanes + new_count]
        best = piece if best is None else jnp.maximum(best, piece)
    best_ref[...] = best


def shards(embeddings, cluster_of, new_rows, centroids):
    clu_count = lax.axis_size("clu")
    rows, width = embeddings.shape
    new_count = new_rows.shape[0]
    cap = 2 * rows // clu_count
    slots = clu_count * cap
    assert slots == chunk_count * lanes
    assert lax.axis_size("grp") == 4
    vmem = pl.BlockSpec(memory_space=pltpu.VMEM)
    anywhere = pl.BlockSpec(memory_space=pl.ANY)
    dma = pltpu.SemaphoreType.DMA
    group_rows = clu_count * new_count
    stage_rows = 2 * lanes
    dup, best = pl.pallas_call(
        functools.partial(exchange_kernel, clu_count, cap, new_count),
        out_shape=(
            jax.ShapeDtypeStruct((1, rows), jnp.float32),
            jax.ShapeDtypeStruct((1, new_count), jnp.float32),
        ),
        in_specs=[anywhere] * 4,
        out_specs=(vmem, vmem),
        scratch_shapes=[
            pltpu.VMEM((rows, width), jnp.bfloat16),
            pltpu.VMEM((1, rows), jnp.int32),
            pltpu.VMEM((new_count, width), jnp.bfloat16),
            pltpu.VMEM(centroids.shape, jnp.bfloat16),
            pltpu.VMEM((rows, width), jnp.bfloat16),
            pltpu.VMEM((slots, width), jnp.bfloat16),
            pltpu.VMEM((clu_count, 1, lanes), jnp.float32),
            pltpu.VMEM((3 * slots, width), jnp.bfloat16),
            pltpu.VMEM((3, clu_count, 1, lanes), jnp.float32),
            pltpu.VMEM((3 * slots, lanes), jnp.float32),
            pltpu.VMEM((stage_count, 2, 8, stage_rows), jnp.float32),
            pltpu.VMEM((stage_count, 8, stage_rows), jnp.float32),
            pltpu.VMEM((stage_count, 8, stage_rows), jnp.float32),
            pltpu.VMEM((stage_count, 8, stage_rows), jnp.float32),
            pltpu.VMEM((4, group_rows, width), jnp.bfloat16),
            pltpu.VMEM(centroids.shape, jnp.bfloat16),
            pltpu.VMEM((4, 8, lanes), jnp.float32),
            pltpu.VMEM((3, 8, lanes), jnp.float32),
            pltpu.VMEM((chunk_count, 1 + group_rows // lanes, lanes), jnp.float32),
            pltpu.VMEM((clu_count, 1 + group_rows // lanes, lanes), jnp.float32),
            dma((4,)),
            dma((clu_count,)),
            dma((clu_count,)),
            dma((clu_count,)),
            dma((clu_count,)),
            dma((clu_count,)),
            dma((clu_count,)),
            dma((2 * chunk_count,)),
            dma((2 * chunk_count,)),
            dma((2 * chunk_count,)),
            dma((2 * chunk_count,)),
            dma((3,)),
            dma((3,)),
            dma((3,)),
            dma((3,)),
            dma((1,)),
            dma((1,)),
            dma((clu_count,)),
            dma((clu_count,)),
        ],
        compiler_params=pltpu.CompilerParams(
            collective_id=0, has_side_effects=True, vmem_limit_bytes=67043328
        ),
        name="exchange",
    )(embeddings, cluster_of.reshape(1, rows), new_rows, centroids)
    return (dup.reshape(rows), best.reshape(new_count))


def solution(mesh):
    return jax.shard_map(
        shards,
        mesh=mesh,
        in_specs=(
            P(("clu", "grp"), None),
            P(("clu", "grp")),
            P(("clu", "grp"), None),
            P(("clu", "grp"), None),
        ),
        out_specs=(P(("clu", "grp")), P(("clu", "grp"))),
        check_vma=False,
    )
```

```python
import functools

import jax
import jax.numpy as jnp
from jax import lax
from jax.experimental import pallas as pl
from jax.experimental.pallas import tpu as pltpu
from jax.sharding import PartitionSpec as P

epsilon = 1e-06
lanes = 128
chunk_order = (0, 1, 2, 3, 4, 5, 6, 7)
chunk_count = len(chunk_order)
stage_count = chunk_count // 2
MESH = pl.DeviceIdType.MESH


def normalize(values):
    wide = values.astype(jnp.float32)
    total = jnp.sum(wide * wide, axis=-1, keepdims=True)
    return (wide * lax.rsqrt(total + epsilon)).astype(jnp.bfloat16)


def pair_scores(left_units, right_units):
    return lax.dot_general(
        left_units, right_units, (((1,), (1,)), ((), ())), preferred_element_type=jnp.float32
    )


def exchange_kernel(
    clu_count,
    cap,
    new_count,
    emb_hbm,
    cluster_hbm,
    new_hbm,
    cent_hbm,
    dup_ref,
    best_ref,
    emb_ref,
    cluster_ref,
    new_ref,
    cent_ref,
    units,
    send_ref,
    ids_ref,
    held,
    held_ids,
    marks,
    id_rows,
    own_acc,
    mate_acc,
    mate_in,
    new_held,
    cent_unit,
    part,
    part_in,
    message,
    message_in,
    local_sem,
    data_send,
    data_recv,
    id_send,
    id_recv,
    new_send,
    new_recv,
    fwd_send,
    fwd_recv,
    fwd_id_send,
    fwd_id_recv,
    wide_send,
    wide_recv,
    part_send,
    part_recv,
    mate_send,
    mate_recv,
    msg_send,
    msg_recv,
):
    per_chunk = clu_count // chunk_count
    half = lanes
    stage_rows = 2 * half
    me = lax.axis_index("clu")
    grp = lax.axis_index("grp")

    def far(block):
        chunk, inner = divmod(block, per_chunk)
        return {"clu": me ^ (chunk_order[chunk] * per_chunk + inner), "grp": grp}

    def near(step):
        return {"clu": me, "grp": grp ^ step}

    def chunk_row(chunk, kind):
        stage, part_of = divmod(chunk, 2)
        return stage * 3 * stage_rows + kind * stage_rows + part_of * half

    def block_rows(block):
        chunk, inner = divmod(block, per_chunk)
        return pl.ds(chunk_row(chunk, 0) + inner * cap, cap)

    def remote(src, dst, send_sem, recv_sem, device):
        return pltpu.make_async_remote_copy(
            src_ref=src,
            dst_ref=dst,
            send_sem=send_sem,
            recv_sem=recv_sem,
            device_id=device,
            device_id_type=MESH,
        )

    barrier = pltpu.get_barrier_semaphore()
    for block in range(1, clu_count):
        pl.semaphore_signal(barrier, inc=1, device_id=far(block), device_id_type=MESH)
    for step in (1, 2, 3):
        pl.semaphore_signal(barrier, inc=1, device_id=near(step), device_id_type=MESH)

    local = [
        pltpu.make_async_copy(new_hbm, new_ref, local_sem.at[0]),
        pltpu.make_async_copy(cluster_hbm, cluster_ref, local_sem.at[1]),
        pltpu.make_async_copy(emb_hbm, emb_ref, local_sem.at[2]),
        pltpu.make_async_copy(cent_hbm, cent_ref, local_sem.at[3]),
    ]
    for copy in local:
        copy.start()

    new_copies = []
    data_copies = [None]
    id_copies = [None]
    for block in range(1, clu_count):
        new_copies.append(
            remote(
                new_held.at[0, pl.ds(0, new_count)],
                new_held.at[0, pl.ds(block * new_count, new_count)],
                new_send.at[block],
                new_recv.at[block],
                far(block),
            )
        )
        id_copies.append(
            remote(
                ids_ref.at[block],
                held_ids.at[0, block],
                id_send.at[block],
                id_recv.at[block],
                far(block),
            )
        )
        data_copies.append(
            remote(
                send_ref.at[pl.ds(block * cap, cap)],
                held.at[block_rows(block)],
                data_send.at[block],
                data_recv.at[block],
                far(block),
            )
        )

    local[0].wait()
    new_held[0, 0:new_count, :] = normalize(new_ref[...])
    local[1].wait()
    cluster = cluster_ref[...]
    rows = cluster.shape[1]
    distance = (cluster & (clu_count - 1)) ^ me
    far_chunk = distance // per_chunk
    place = jnp.zeros_like(distance)
    for index, chunk in enumerate(chunk_order):
        place = jnp.where(far_chunk == chunk, index, place)
    place = place * per_chunk + distance % per_chunk
    owner_hot = lax.broadcasted_iota(jnp.int32, (clu_count, rows), 0) == place
    before = lax.broadcasted_iota(jnp.int32, (rows, rows), 0) < lax.broadcasted_iota(
        jnp.int32, (rows, rows), 1
    )
    preceding = jnp.dot(
        owner_hot.astype(jnp.bfloat16),
        before.astype(jnp.bfloat16),
        preferred_element_type=jnp.float32,
    )
    rank = jnp.sum(jnp.where(owner_hot, preceding, 0.0), axis=0, keepdims=True).astype(jnp.int32)
    slot = place * cap + rank
    id_values = jnp.broadcast_to((cluster + 1).astype(jnp.float32), (8, rows)).astype(jnp.bfloat16)
    chunk_slot = lax.broadcasted_iota(jnp.int32, (lanes, rows), 0)
    inner_block = lax.broadcasted_iota(jnp.int32, (1, lanes), 1) // cap
    local[2].wait()
    units[...] = normalize(emb_ref[...])
    def pack(chunk):
        chosen = (chunk_slot + chunk * lanes == slot).astype(jnp.bfloat16)
        packed = jnp.dot(chosen, units[...], preferred_element_type=jnp.float32).astype(
            jnp.bfloat16
        )
        tile = pair_scores(id_values, chosen)[0:1]
        for inner in range(per_chunk):
            block = chunk * per_chunk + inner
            if per_chunk == 1:
                own_tile = tile
            else:
                own_tile = jnp.where(inner_block == inner, tile, 0.0)
            if block == 0:
                held_ids[0, 0] = own_tile
                held[block_rows(0), :] = packed[0:cap]
            else:
                ids_ref[block] = own_tile
        if per_chunk > 1 or chunk > 0:
            send_ref[chunk * lanes : (chunk + 1) * lanes, :] = packed

    def dispatch(chunk):
        for block in range(max(1, chunk * per_chunk), (chunk + 1) * per_chunk):
            id_copies[block].start()
            data_copies[block].start()

    forwards = {}

    def spread_marks(chunk, kind):
        tile = held_ids[kind, chunk * per_chunk]
        for inner in range(1, per_chunk):
            tile = tile + held_ids[kind, chunk * per_chunk + inner]
        square = jnp.broadcast_to(tile, (lanes, lanes))
        marks[pl.ds(chunk_row(chunk, kind), half), :] = jnp.transpose(square)
        if kind < 2:
            stage, part_of = divmod(chunk, 2)
            id_rows[stage, kind, :, pl.ds(part_of * half, half)] = jnp.broadcast_to(
                tile, (8, half)
            )

    def pass_on(chunk):
        for inner in range(per_chunk):
            block = chunk * per_chunk + inner
            if block > 0:
                id_copies[block].wait_recv()
                data_copies[block].wait_recv()
        src_rows = pl.ds(chunk_row(chunk, 0), half)
        src_ids = pl.ds(chunk * per_chunk, per_chunk)
        for kind in (2, 1):
            index = (kind - 1) * chunk_count + chunk
            ids = remote(
                held_ids.at[0, src_ids],
                held_ids.at[kind, src_ids],
                fwd_id_send.at[index],
                fwd_id_recv.at[index],
                near(kind),
            )
            data = remote(
                held.at[src_rows],
                held.at[pl.ds(chunk_row(chunk, kind), half)],
                fwd_send.at[index],
                fwd_recv.at[index],
                near(kind),
            )
            ids.start()
            data.start()
            forwards[chunk, kind] = (ids, data)
        spread_marks(chunk, 0)

    def receive(chunk, kinds=(1, 2)):
        for kind in kinds:
            ids, data = forwards[chunk, kind]
            ids.wait_recv()
            data.wait_recv()
            spread_marks(chunk, kind)

    def fold(scores, matched):
        kept = jnp.where(matched, scores, -1.0)
        return jnp.max(kept.reshape(stage_rows // 8, 8, stage_rows), axis=0)

    def tile_rows(stage, kind):
        start = stage * (3 * stage_rows) + kind * stage_rows
        if not isinstance(start, int):
            start = pl.multiple_of(start, stage_rows)
        return pl.ds(start, stage_rows)

    def own_pair(kind, left, right):
        rows = tile_rows(left, kind)
        mark = marks[rows, :]
        matched = jnp.concatenate([mark, mark], axis=1) == id_rows[right, 0][0:1]
        if kind == 0:
            row_id = lax.broadcasted_iota(jnp.int32, (stage_rows, stage_rows), 0)
            col_id = lax.broadcasted_iota(jnp.int32, (stage_rows, stage_rows), 1)
            matched = matched & (row_id - col_id != (right - left) * stage_rows)
        scores = pair_scores(held[rows, :], held[tile_rows(right, 0), :])
        own_acc[right] = jnp.maximum(own_acc[right], fold(scores, matched))

    def mate_pair(left, right):
        rows = tile_rows(left, 2)
        mark = marks[rows, :]
        matched = jnp.concatenate([mark, mark], axis=1) == id_rows[right, 1][0:1]
        scores = pair_scores(held[rows, :], held[tile_rows(right, 1), :])
        mate_acc[right] = jnp.maximum(mate_acc[right], fold(scores, matched))

    def compute(stage):
        receive(2 * stage)
        receive(2 * stage + 1)

        def body(step, carry):
            left = jnp.minimum(step, stage)
            right = jnp.where(step <= stage, stage, step - stage - 1)
            for kind in range(3):
                own_pair(kind, left, right)
            mate_pair(left, right)
            return carry

        lax.fori_loop(0, 2 * stage + 1, body, 0)

    def compute_last():
        last = stage_count - 1

        def own_rows(step, carry):
            own_pair(0, last, step)
            return carry

        def own_cols(step, carry):
            for kind in range(3):
                own_pair(kind, step, last)
            return carry

        def mate_rows(step, carry):
            own_pair(1, last, step)
            return carry

        def cross_rows(step, carry):
            own_pair(2, last, step)
            mate_pair(last, step)
            return carry

        def mate_cols(step, carry):
            mate_pair(step, last)
            return carry

        lax.fori_loop(0, stage_count, own_rows, 0)
        lax.fori_loop(0, last, own_cols, 0)
        receive(2 * last, (1,))
        receive(2 * last + 1, (1,))
        lax.fori_loop(0, last, mate_cols, 0)
        lax.fori_loop(0, stage_count, mate_rows, 0)
        receive(2 * last, (2,))
        receive(2 * last + 1, (2,))
        lax.fori_loop(0, stage_count, cross_rows, 0)

    group_rows = clu_count * new_count
    best_rows = group_rows // lanes
    cross_new = remote(
        new_held.at[0], new_held.at[2], wide_send.at[0], wide_recv.at[0], near(2)
    )
    mate_new = remote(new_held.at[0], new_held.at[1], wide_send.at[1], wide_recv.at[1], near(1))
    corner_new = remote(new_held.at[2], new_held.at[3], wide_send.at[2], wide_recv.at[2], near(1))
    part_copies = [
        remote(
            part.at[step],
            part_in.at[step - 1],
            part_send.at[step - 1],
            part_recv.at[step - 1],
            near(step),
        )
        for step in (1, 2, 3)
    ]

    def new_first():
        for copy in new_copies:
            copy.wait_recv()
        cross_new.start()
        mate_new.start()

    def new_second():
        cross_new.wait_recv()
        corner_new.start()

    def new_third():
        mate_new.wait_recv()
        corner_new.wait_recv()
        for step in range(4):
            scores = pair_scores(cent_unit[...], new_held[step])
            top = jnp.max(
                scores.reshape(scores.shape[0] // 8, 8, group_rows), axis=0
            )
            top = jnp.max(top, axis=0, keepdims=True)
            if group_rows == lanes:
                part[step] = jnp.broadcast_to(top, (8, lanes))
            else:
                for row in range(group_rows // lanes):
                    part[step, row : row + 1, :] = top[:, row * lanes : (row + 1) * lanes]
        for copy in part_copies:
            copy.start()

    for chunk in range(chunk_count):
        pack(chunk)
    pl.semaphore_wait(barrier, clu_count - 1 + 3)
    for copy in new_copies:
        copy.start()
    for chunk in (0, 1, 2, 3, 4):
        dispatch(chunk)
    own_acc[...] = jnp.full(own_acc.shape, -1.0, jnp.float32)
    mate_acc[...] = jnp.full(mate_acc.shape, -1.0, jnp.float32)
    pass_on(0)
    local[3].wait()
    cent_unit[...] = normalize(cent_ref[...])
    pass_on(1)
    dispatch(5)
    new_first()
    pass_on(2)
    pass_on(3)
    dispatch(6)
    new_second()
    compute(0)
    pass_on(4)
    dispatch(7)
    new_third()
    pass_on(5)
    compute(1)
    pass_on(6)
    compute(2)
    pass_on(7)
    compute_last()

    mate_copy = remote(mate_acc, mate_in, mate_send.at[0], mate_recv.at[0], near(1))
    mate_copy.start()
    cent_best = part[0]
    for step in (1, 2, 3):
        part_copies[step - 1].wait_recv()
        cent_best = jnp.maximum(cent_best, part_in[step - 1])
    mate_copy.wait_recv()
    for stage in range(stage_count):
        final = jnp.max(
            jnp.maximum(own_acc[stage], mate_in[stage]), axis=0, keepdims=True
        )
        for part_of in range(2):
            message[2 * stage + part_of, 0:1, :] = final[:, part_of * half : (part_of + 1) * half]
            message[2 * stage + part_of, 1:, :] = cent_best[0:best_rows]
    messages = []
    for block in range(1, clu_count):
        copy = remote(
            message.at[block // per_chunk],
            message_in.at[block],
            msg_send.at[block],
            msg_recv.at[block],
            far(block),
        )
        copy.start()
        messages.append(copy)
    message_in[0] = message[0]
    for block in range(1, clu_count):
        new_copies[block - 1].wait_send()
        id_copies[block].wait_send()
        data_copies[block].wait_send()
    for ids, data in forwards.values():
        ids.wait_send()
        data.wait_send()
    for copy in (cross_new, mate_new, corner_new, mate_copy, *part_copies):
        copy.wait_send()
    for copy in messages:
        copy.wait()

    lane_block = lax.broadcasted_iota(jnp.int32, (1, lanes), 1) // cap
    row_list = []
    for chunk in range(chunk_count):
        row = message_in[chunk * per_chunk, 0:1, :]
        for inner in range(1, per_chunk):
            row = jnp.where(lane_block == inner, message_in[chunk * per_chunk + inner, 0:1, :], row)
        row_list.append(row)
    columns = jnp.transpose(
        jnp.concatenate([jnp.broadcast_to(row, (16, lanes)) for row in row_list], axis=0)
    )
    total = jnp.zeros(slot.shape, jnp.float32)
    position = lax.broadcasted_iota(jnp.int32, (lanes, slot.shape[1]), 0)
    for chunk in range(chunk_count):
        column = columns[:, chunk * 16 : chunk * 16 + 1]
        total = total + jnp.sum(
            jnp.where(position + chunk * lanes == slot, column, 0.0), axis=0, keepdims=True
        )
    dup_ref[...] = total
    best = None
    for block in range(clu_count):
        start = block * new_count
        row = 1 + start // lanes
        piece = message_in[block, row : row + 1, :][:, start % lanes : start % lanes + new_count]
        best = piece if best is None else jnp.maximum(best, piece)
    best_ref[...] = best


def shards(embeddings, cluster_of, new_rows, centroids):
    clu_count = lax.axis_size("clu")
    rows, width = embeddings.shape
    new_count = new_rows.shape[0]
    cap = 2 * rows // clu_count
    slots = clu_count * cap
    assert slots == chunk_count * lanes
    assert lax.axis_size("grp") == 4
    vmem = pl.BlockSpec(memory_space=pltpu.VMEM)
    anywhere = pl.BlockSpec(memory_space=pl.ANY)
    dma = pltpu.SemaphoreType.DMA
    group_rows = clu_count * new_count
    stage_rows = 2 * lanes
    dup, best = pl.pallas_call(
        functools.partial(exchange_kernel, clu_count, cap, new_count),
        out_shape=(
            jax.ShapeDtypeStruct((1, rows), jnp.float32),
            jax.ShapeDtypeStruct((1, new_count), jnp.float32),
        ),
        in_specs=[anywhere] * 4,
        out_specs=(vmem, vmem),
        scratch_shapes=[
            pltpu.VMEM((rows, width), jnp.bfloat16),
            pltpu.VMEM((1, rows), jnp.int32),
            pltpu.VMEM((new_count, width), jnp.bfloat16),
            pltpu.VMEM(centroids.shape, jnp.bfloat16),
            pltpu.VMEM((rows, width), jnp.bfloat16),
            pltpu.VMEM((slots, width), jnp.bfloat16),
            pltpu.VMEM((clu_count, 1, lanes), jnp.float32),
            pltpu.VMEM((3 * slots, width), jnp.bfloat16),
            pltpu.VMEM((3, clu_count, 1, lanes), jnp.float32),
            pltpu.VMEM((3 * slots, lanes), jnp.float32),
            pltpu.VMEM((stage_count, 2, 8, stage_rows), jnp.float32),
            pltpu.VMEM((stage_count, 8, stage_rows), jnp.float32),
            pltpu.VMEM((stage_count, 8, stage_rows), jnp.float32),
            pltpu.VMEM((stage_count, 8, stage_rows), jnp.float32),
            pltpu.VMEM((4, group_rows, width), jnp.bfloat16),
            pltpu.VMEM(centroids.shape, jnp.bfloat16),
            pltpu.VMEM((4, 8, lanes), jnp.float32),
            pltpu.VMEM((3, 8, lanes), jnp.float32),
            pltpu.VMEM((chunk_count, 1 + group_rows // lanes, lanes), jnp.float32),
            pltpu.VMEM((clu_count, 1 + group_rows // lanes, lanes), jnp.float32),
            dma((4,)),
            dma((clu_count,)),
            dma((clu_count,)),
            dma((clu_count,)),
            dma((clu_count,)),
            dma((clu_count,)),
            dma((clu_count,)),
            dma((2 * chunk_count,)),
            dma((2 * chunk_count,)),
            dma((2 * chunk_count,)),
            dma((2 * chunk_count,)),
            dma((3,)),
            dma((3,)),
            dma((3,)),
            dma((3,)),
            dma((1,)),
            dma((1,)),
            dma((clu_count,)),
            dma((clu_count,)),
        ],
        compiler_params=pltpu.CompilerParams(
            collective_id=0, has_side_effects=True, vmem_limit_bytes=67043328
        ),
        name="exchange",
    )(embeddings, cluster_of.reshape(1, rows), new_rows, centroids)
    return (dup.reshape(rows), best.reshape(new_count))


def solution(mesh):
    return jax.shard_map(
        shards,
        mesh=mesh,
        in_specs=(
            P(("clu", "grp"), None),
            P(("clu", "grp")),
            P(("clu", "grp"), None),
            P(("clu", "grp"), None),
        ),
        out_specs=(P(("clu", "grp")), P(("clu", "grp"))),
        check_vma=False,
    )
```
